32 devices in a mesh: group: 4 (over y, core), blk: 8 (over z, x).
Axes of the slice: x: 2, y: 2, z: 4, core: 2. Of those that a mesh axis runs over, the one named last changes fastest.
Arguments:
- features: bfloat16 [1024, 2048], P('blk', 'group'), may hold values from -6 to 6
- weight: bfloat16 [2048, 256], P('group'), may hold values from -0.125 to 0.125
- queue: bfloat16 [16384, 256], P(('group', 'blk')), may hold values from -0.5 to 0.5, as said below
- fresh_keys: bfloat16 [1024, 256], P('blk'), may hold values from -0.3984375 to 0.3984375
- positives: int32 [1024], P('blk'), may hold values from 0 to 1023, each once
- write_slot: int32 [1], replicated, may hold values from 0 to 15360
Outputs:
- query_loss: float32 [1024], P('blk')
- weight_grad: float32 [2048, 256], P(('group', 'blk'))
- new_queue: bfloat16 [16384, 256], P(('group', 'blk'))
The draws below stay inside these ranges and needn't reach their ends.
Inputs may be any that keep to these rules, and one draw needn't show every extreme that they name: `queue`: scaled item keys.
All inputs are finite; a program needn't handle non-finite values.
Results may differ from the reference program's by a relative error of at most 0.003.
The reference program's roundings to bfloat16 on the way count: a program that leaves them out, or rounds other values in their place, can miss the bound.
Values may be sent and summed in bfloat16 or wider, within the bound.
No kernel may reach another device: no remote copies, remote signals or barrier semaphores. Data moves between devices by JAX's collectives and lax.ppermute only.
A program may use at most 64 MiB of HBM per device.

```python
import math
import jax
import jax.numpy as jnp
from jax import lax

WIDTH = 256
FEATURES = 2048
SLOT_ROWS = 512
QUERIES = 1024
SLOTS = 16384


def draw_queue(key, part):
    key_scale = jax.random.fold_in(key, 11)
    key_entries = jax.random.fold_in(key, 12)
    key_assign = jax.random.fold_in(key, 14)
    key_centres = jax.random.fold_in(key, 15)
    key_device = jax.random.fold_in(key, 16)
    centre_count = 128
    root = math.sqrt(WIDTH)
    device_total = SLOTS // SLOT_ROWS
    device_scale = jnp.exp(jax.random.uniform(key_device, (device_total, 1, 1), jnp.float32, math.log(0.4), math.log(2.5)))
    device_scale = jnp.broadcast_to(device_scale, (device_total, SLOT_ROWS, 1)).reshape(SLOTS, 1)
    scales = jnp.exp(jax.random.uniform(key_scale, (SLOTS, 1), jnp.float32, math.log(0.25), math.log(2.5)))
    rising = 0.8 + 0.4 * jnp.arange(SLOTS, dtype=jnp.float32)[:, None] / SLOTS
    centres = jax.random.normal(key_centres, (centre_count, WIDTH), jnp.float32)
    centres = centres / jnp.sqrt(jnp.sum(centres * centres, axis=1, keepdims=True))
    assign = jax.random.randint(key_assign, (SLOTS,), 0, centre_count)
    members = jnp.take(centres, assign, axis=0)
    noise = jax.random.normal(key_entries, (SLOTS, WIDTH), jnp.float32) / root
    entries = 0.9 * members + 0.45 * noise
    entries = jnp.clip(entries * scales * rising * device_scale, -0.5, 0.5)
    return entries.astype(jnp.bfloat16)


def spiked(drawn, stream_key, source, target, blocks, factor):
    owner, partner = [(jnp.arange(drawn.shape[axis_at]) // (drawn.shape[axis_at] // blocks)).reshape([-1 if axis == axis_at else 1 for axis in range(drawn.ndim)]) for axis_at in (source, target)]
    chosen = jax.random.permutation(stream_key, blocks)[partner]
    strong = (owner == chosen) | (owner == (partner + blocks // 2) % blocks)
    return jnp.where(strong, factor * drawn, drawn)


def block_levels(rng, dims, shards, smallest, high):
    def one(dim, parts):
        heights = jax.random.uniform(jax.random.fold_in(jax.random.fold_in(rng, 6), dim), (parts,), jnp.float32, smallest / len(shards), high / len(shards))
        return jnp.repeat(jnp.exp(heights), dims[dim] // parts).reshape((-1,) + (1,) * (len(dims) - dim - 1))

    factor_of = one(*shards[0])
    for cut in shards[1:]:
        factor_of = factor_of * one(*cut)
    return factor_of


def normal_values(own_key, dims, scale, reach, pieces=(), kind=jnp.bfloat16):
    array = jax.random.normal(own_key, dims, jnp.float32) * scale
    if len(pieces) > 0:
        array = block_levels(own_key, dims, pieces, -0.22, 0.18) * array
    return jnp.clip(array, min=-reach, max=reach).astype(kind)


def gaussian_with(key, dims, width, limit, pieces, heavy, held_as=jnp.bfloat16):
    values = width * jax.random.normal(key, dims, jnp.float32)
    if pieces:
        values = values * block_levels(key, dims, pieces, -0.22, 0.18)
    return jnp.clip(spiked(values, jax.random.fold_in(key, 3), *heavy), -limit, limit).astype(held_as)


def setup_inputs(seed: int = 0) -> dict:
    arg_keys = jax.random.split(jax.random.key(seed), 7)
    features = gaussian_with(arg_keys[0], (QUERIES, FEATURES), 1.0, 6.0, ((0, 8), (1, 4)), (0, 1, 8, 2.0))
    weight = normal_values(arg_keys[1], (FEATURES, WIDTH), FEATURES ** -0.5, 0.125, ((0, 4),))
    queue = draw_queue(jax.random.fold_in(arg_keys[6], 71), 0)
    fresh_keys = normal_values(arg_keys[3], (QUERIES, WIDTH), 0.0625, 0.3984375, ((0, 8),))
    positives = jax.random.permutation(arg_keys[4], QUERIES).astype(jnp.int32)
    write_slot = jax.random.randint(arg_keys[5], (1,), 0, SLOTS - QUERIES + 1).astype(jnp.int32)
    return {"features": features, "weight": weight, "queue": queue, "fresh_keys": fresh_keys, "positives": positives, "write_slot": write_slot}


epsilon = 1e-06
inverse_sharpness_factor = 8.0

def reference(features, weight, queue, fresh_keys, positives, write_slot):
    projected = jnp.dot(features, weight, preferred_element_type=jnp.float32)
    length = jnp.sqrt(lax.optimization_barrier(jnp.sum(projected * projected, axis=1, keepdims=True)) + epsilon)
    unit_rows = projected / length
    query_rows = unit_rows.astype(jnp.bfloat16)
    block_rows = 8192 if SLOTS % 8192 == 0 else SLOTS
    key_blocks = queue.reshape(SLOTS // block_rows, block_rows, WIDTH)

    def score_step(carry, keys):
        numerator, denominator = carry
        similarity_matrix = jnp.dot(query_rows, keys.T, preferred_element_type=jnp.float32)
        exponentials = jnp.exp(inverse_sharpness_factor * similarity_matrix)
        denominator = denominator + lax.optimization_barrier(jnp.sum(exponentials, axis=1))
        numerator = numerator + jnp.dot(exponentials.astype(jnp.bfloat16), keys, preferred_element_type=jnp.float32)
        return ((numerator, denominator), None)
    start_sums = (jnp.zeros((QUERIES, WIDTH), jnp.float32), jnp.zeros((QUERIES,), jnp.float32))
    (numerator, denominator), _ = lax.scan(score_step, start_sums, key_blocks)
    paired_encodings = jnp.take(fresh_keys, positives, axis=0).astype(jnp.float32)
    pair_score = inverse_sharpness_factor * lax.optimization_barrier(jnp.sum(query_rows.astype(jnp.float32) * paired_encodings, axis=1))
    pair_weight = jnp.exp(pair_score)
    probability_mass = pair_weight + denominator
    query_loss = jnp.log(probability_mass) - pair_score
    query_derivative = inverse_sharpness_factor * ((pair_weight[:, None] * paired_encodings + numerator) / probability_mass[:, None] - paired_encodings)
    along = lax.optimization_barrier(jnp.sum(query_derivative * unit_rows, axis=1, keepdims=True))
    grad_projected = ((query_derivative - along * unit_rows) / length).astype(jnp.bfloat16)
    weight_grad = jnp.dot(features.T, grad_projected, preferred_element_type=jnp.float32)
    window_start = write_slot[0].astype(jnp.int32)
    new_queue = lax.dynamic_update_slice(queue, fresh_keys, (window_start, jnp.int32(0)))
    return (query_loss, weight_grad, new_queue)
```

```python
import functools
import jax
import jax.numpy as jnp
from jax import lax
from jax.experimental import pallas as pl
from jax.experimental.pallas import tpu as pltpu
from jax.sharding import PartitionSpec as P


epsilon = 1e-06
inverse_sharpness_factor = 8.0
f32, bf16 = jnp.float32, jnp.bfloat16
VMEM = pl.BlockSpec(memory_space=pltpu.VMEM)
SMEM = pl.BlockSpec(memory_space=pltpu.SMEM)


def call(body, outs, ins, name, flops=0):
    nbytes = sum(a.size * a.dtype.itemsize for a in ins) + sum(o.size * o.dtype.itemsize for o in outs)
    return pl.pallas_call(
        body,
        out_shape=outs,
        in_specs=[SMEM] + [VMEM] * (len(ins) - 1),
        out_specs=[VMEM] * len(outs),
        name=name,
        cost_estimate=pl.CostEstimate(flops=flops, bytes_accessed=nbytes, transcendentals=0),
    )(*ins)


def shape(*dims, dtype=f32):
    return jax.ShapeDtypeStruct(dims, dtype)


def dot(a, b):
    return jnp.dot(a, b, preferred_element_type=f32)


def row_block(lo_row, hi_row):
    n = lo_row.shape[1]
    first = lax.broadcasted_iota(jnp.int32, (16, n), 0) == 0
    parts = [jnp.where(first, jnp.broadcast_to(v, (16, n)), 0.0).astype(bf16) for v in (lo_row, hi_row)]
    return jnp.concatenate(parts, axis=1)


def split_row(row):
    high = row.astype(bf16).astype(f32)
    return high, row - high


def as_row(col):
    n = col.shape[0]
    return jnp.transpose(jnp.broadcast_to(col, (n, n)))[0:1, :]


def as_column(row):
    n = row.shape[1]
    return jnp.transpose(jnp.broadcast_to(row, (n, n)))[:, 0:1]


def prep_body(ids, features, weight, fresh, positives, keep, send, *rest):
    messages, scratch = rest[:-1], rest[-1]
    z, core = ids[0], ids[1]
    rows, width = fresh.shape
    half = rows // 2
    scratch[...] = dot(features[...], weight[...])
    keep[...] = scratch[pl.ds(pl.multiple_of(core * half, half), half), :]
    send[...] = scratch[pl.ds(pl.multiple_of((1 - core) * half, half), half), :]
    cols = features.shape[1] // (len(messages) + 1)
    index = positives[...]
    tail = row_block(
        lax.shift_right_logical(index, 7).astype(f32), lax.bitwise_and(index, 127).astype(f32)
    )
    for k, message in enumerate(messages, 1):
        peer = lax.bitwise_xor(z, k)
        message[0:rows, 0:width] = fresh[...]
        message[0:rows, width:] = features[:, pl.ds(pl.multiple_of(peer * cols, cols), cols)]
        message[rows:, 0:width] = tail
        message[rows:, width:] = jnp.zeros((16, cols), bf16)


def halve_body(ids, keep, got, own, send):
    quarter = own.shape[0]
    y = ids[0]
    for ref, at in ((own, y), (send, 1 - y)):
        rows = pl.ds(pl.multiple_of(at * quarter, quarter), quarter)
        ref[...] = keep[rows, :] + got[rows, :]


def pack_pair(first, second, x):
    half = first.shape[1] // 2
    low = jnp.concatenate([first[:, :half], second[:, :half]], axis=1)
    high = jnp.concatenate([first[:, half:], second[:, half:]], axis=1)
    return jnp.where(x == 0, low, high)


def feature_blocks(ids, features, messages, rows, width):
    z = ids[0]
    cols = features.shape[1] // (len(messages) + 1)
    own = features[:, pl.ds(pl.multiple_of(z * cols, cols), cols)]
    return [own.astype(f32)] + [m[0:rows, width:].astype(f32) for m in messages]


def cross_body(ids, features, fresh, *rest):
    messages, out = rest[:-1], rest[-1]
    rows, width = fresh.shape
    other = 1 - ids[1]
    blocks = feature_blocks(ids, features, messages, rows, width)
    for k, ref in enumerate((fresh, *messages)):
        out[:, k * width : (k + 1) * width] = ref[0:rows, 0:width]
    base = len(blocks) * width
    lanes = blocks[0].shape[1]
    for k in range(0, len(blocks), 2):
        pair = pack_pair(blocks[k], blocks[k + 1], other).astype(bf16)
        out[:, base + k // 2 * lanes : base + (k // 2 + 1) * lanes] = pair


def arrange_body(ids, features, fresh, *rest):
    messages, crossed, out, scratch = rest[:-3], rest[-3], rest[-2], rest[-1]
    rows, width = fresh.shape
    x, y, core = ids[1], ids[2], ids[3]
    quarter = rows // 4
    blocks = feature_blocks(ids, features, messages, rows, width)
    lanes = blocks[0].shape[1]
    base = len(blocks) * width
    per_z = 8 * quarter
    for k in range(0, len(blocks), 2):
        scratch[0] = pack_pair(blocks[k], blocks[k + 1], x)
        scratch[1] = crossed[:, base + k // 2 * lanes : base + (k // 2 + 1) * lanes].astype(f32)
        picked = []
        for dx in range(2):
            for dy in range(2):
                for dc in range(2):
                    at = lax.bitwise_xor(core, dc) * 2 + lax.bitwise_xor(y, dy)
                    picked.append(scratch[dx, pl.ds(pl.multiple_of(at * quarter, quarter), quarter), :])
        turned = jnp.transpose(jnp.concatenate(picked, axis=0)).astype(bf16)
        out[:, k * per_z : (k + 1) * per_z] = turned[0 : lanes // 2]
        out[:, (k + 1) * per_z : (k + 2) * per_z] = turned[lanes // 2 :]


def unit_of(projected):
    length = jnp.sqrt(jnp.sum(projected * projected, axis=1, keepdims=True) + epsilon)
    return projected / length, length


def score_body(ids, *refs):
    queries, keys, (message, numer_out, denom_out) = refs[:4], refs[4:-3], refs[-3:]
    projected = jnp.concatenate([q[...] for q in queries], axis=0)
    query = unit_of(projected)[0].astype(bf16)
    count, width = projected.shape
    numer = jnp.zeros((count, width), f32)
    denom = jnp.zeros((count, 1), f32)
    for block in keys:
        key = block[...]
        similarity = lax.dot_general(query, key, (((1,), (1,)), ((), ())), preferred_element_type=f32)
        e = jnp.exp(inverse_sharpness_factor * similarity)
        denom = denom + jnp.sum(e, axis=1, keepdims=True)
        numer = numer + dot(e.astype(bf16), key)
    numer_out[...] = numer
    denom_out[...] = jnp.broadcast_to(denom, denom_out.shape)
    message[0:count, :] = numer.astype(bf16)
    message[count:, :] = row_block(*split_row(as_row(denom)))


def grad_body(ids, *refs):
    queries, numer_ref, denom_ref = refs[:4], refs[4], refs[5]
    messages, (positives, fresh), blocks, crossed, out = refs[6:9], refs[9:11], refs[11:14], refs[14], refs[15]
    z, x, quarter_at = ids[0], ids[1], ids[4]
    projected = jnp.concatenate([q[...] for q in queries], axis=0)
    count, width = projected.shape
    quarter = count // 4
    unit, length = unit_of(projected)
    query = unit.astype(bf16).astype(f32)
    numer = numer_ref[...]
    denom = denom_ref[:, 0:1]
    for j, message in enumerate(messages, 1):
        part = message[0:count, :].astype(f32)
        row = message[count : count + 16, :].astype(f32)[0:1, :]
        column = as_column(row[:, :count] + row[:, count:])
        order = [j ^ k for k in range(4)]
        numer = numer + jnp.concatenate([part[k * quarter : (k + 1) * quarter] for k in order], axis=0)
        denom = denom + jnp.concatenate([column[k * quarter : (k + 1) * quarter] for k in order], axis=0)
    lanes = lax.broadcasted_iota(jnp.int32, (1, count), 1)
    tables = [positives[...].astype(f32)]
    for block in blocks:
        row = block[count : count + 16, 0:width].astype(f32)[0:1, :]
        tables.append(row[:, :count] * 128.0 + row[:, count:])
    columns = []
    for table in tables:
        column = jnp.transpose(jnp.broadcast_to(table, (count, count)))
        picked = jnp.zeros((quarter, 1), f32)
        for at in range(4):
            picked = jnp.where(quarter_at == at, column[at * quarter : (at + 1) * quarter, 0:1], picked)
        columns.append(picked)
    index = jnp.concatenate(columns, axis=0).astype(jnp.int32)
    slots = lax.broadcasted_iota(jnp.int32, (count, count), 1)
    positive = jnp.zeros((count, width), f32)
    for k in range(4):
        for dx in range(2):
            base = (lax.bitwise_xor(z, k) * 2 + lax.bitwise_xor(x, dx)) * count
            hot = (slots + base == index).astype(f32).astype(bf16)
            if dx == 1:
                rows = crossed[:, k * width : (k + 1) * width]
            else:
                rows = fresh[...] if k == 0 else blocks[k - 1][0:count, 0:width]
            positive = positive + dot(hot, rows)
    score = inverse_sharpness_factor * jnp.sum(query * positive, axis=1, keepdims=True)
    weight = jnp.exp(score)
    mass = weight + denom
    loss = jnp.log(mass) - score
    slope = inverse_sharpness_factor * ((weight * positive + numer) / mass - positive)
    along = jnp.sum(slope * unit, axis=1, keepdims=True)
    out[0:count, :] = ((slope - along * unit) / length).astype(bf16)
    out[count:, :] = row_block(*split_row(as_row(loss)))


def final_body(ids, *refs):
    turned, pieces, (grad, loss_out) = refs[0], refs[1:9], refs[9:]
    y, core = ids[2], ids[3]
    count = pieces[0].shape[0] - 16
    quarter = count // 4
    total = None
    for m in range(4):
        rows = jnp.concatenate([p[m * quarter : (m + 1) * quarter, :] for p in pieces], axis=0)
        term = dot(turned[:, m * 8 * quarter : (m + 1) * 8 * quarter], rows)
        total = term if total is None else total + term
    grad[...] = total
    place = lax.broadcasted_iota(jnp.int32, (1, count), 1) // quarter
    loss = jnp.zeros((1, count), f32)
    for dy in range(2):
        for dc in range(2):
            row = pieces[dy * 2 + dc][count : count + 16, :].astype(f32)[0:1, :]
            value = (row[:, :count] + row[:, count:])[:, :quarter]
            at = lax.bitwise_xor(core, dc) * 2 + lax.bitwise_xor(y, dy)
            loss = jnp.where(place == at, jnp.concatenate([value] * 4, axis=1), loss)
    loss_out[...] = loss


def enqueue_body(ids, queue, fresh, m1, m2, m3, crossed, out, scratch):
    z, x, start = ids[0], ids[1], ids[5]
    slots, width = queue.shape
    rows = fresh.shape[0]
    total = 8 * rows
    out[...] = queue[...]
    @pl.when((start < total) & (start + slots > 0))
    def _():
        scratch[...] = jnp.zeros((slots, width), f32)
        offset = lax.broadcasted_iota(jnp.int32, (slots, rows), 0) + start
        place = lax.broadcasted_iota(jnp.int32, (slots, rows), 1)
        for k in range(4):
            for dx in range(2):
                base = (lax.bitwise_xor(z, k) * 2 + lax.bitwise_xor(x, dx)) * rows

                @pl.when((start < base + rows) & (start + slots > base))
                def _():
                    hot = (place + base == offset).astype(f32).astype(bf16)
                    if dx == 1:
                        values = crossed[:, k * width : (k + 1) * width]
                    else:
                        values = fresh[...] if k == 0 else (m1, m2, m3)[k - 1][0:rows, 0:width]
                    scratch[...] += dot(hot, values)

        at = lax.broadcasted_iota(jnp.int32, (slots, width), 0) + start
        inside = (at >= 0) & (at < total)
        out[...] = jnp.where(inside, scratch[...], queue[...].astype(f32)).astype(bf16)


def fast(features, weight, queue, fresh, positives, write_slot):
    group, blk = lax.axis_index("group"), lax.axis_index("blk")
    groups, blks = lax.axis_size("group"), lax.axis_size("blk")
    y, core, z, x = group // 2, group % 2, blk // 2, blk % 2
    rows, width = fresh.shape
    slots = queue.shape[0]
    device = group * blks + blk
    start = device * slots - write_slot[0]
    ids = jnp.stack([z, x, y, core, core * 2 + y, start]).astype(jnp.int32)

    def move(value, dg, db):
        pairs = [
            (g * blks + b, (g ^ dg) * blks + (b ^ db)) for g in range(groups) for b in range(blks)
        ]
        return lax.ppermute(value, ("group", "blk"), pairs)

    keys = [queue] + [move(queue, dy * 2, dx) for dy, dx in ((0, 1), (1, 0), (1, 1))]
    keys += [move(k, 1, 0) for k in keys]

    positives_row = positives.reshape(1, rows)
    prep = pl.pallas_call(
        prep_body,
        out_shape=[shape(rows // 2, width)] * 2 + [shape(rows + 16, width + features.shape[1] // 4, dtype=bf16)] * 3,
        in_specs=[SMEM] + [VMEM] * 4,
        out_specs=[VMEM] * 5,
        scratch_shapes=[pltpu.VMEM((rows, width), f32)],
        name="prep",
        cost_estimate=pl.CostEstimate(flops=2 * rows * width * features.shape[1], bytes_accessed=1 << 20, transcendentals=0),
    )
    keep, send, *outgoing = prep(jnp.stack([z, core]).astype(jnp.int32), features, weight, fresh, positives_row)
    blocks = [move(m, 0, 2 * k) for k, m in enumerate(outgoing, 1)]
    got = move(send, 1, 0)
    own, send = call(halve_body, [shape(rows // 4, width)] * 2, [ids[2:3], keep, got], "halve")
    own = own + move(send, 2, 0)
    queries = [own] + [move(own, 0, 2 * k) for k in (1, 2, 3)]

    crossed = move(
        call(cross_body, [shape(rows, 4 * width + features.shape[1] // 2, dtype=bf16)], [ids, features, fresh, *blocks], "cross")[0],
        0,
        1,
    )
    message, numer, denom = call(
        score_body,
        [shape(rows + 16, width, dtype=bf16), shape(rows, width), shape(rows, rows)],
        [ids, *queries, *keys],
        "score",
        flops=4 * rows * width * 8 * slots,
    )
    received = [move(message, 0, 2 * k) for k in (1, 2, 3)]
    turned = pl.pallas_call(
        arrange_body,
        out_shape=shape(features.shape[1] // 8, 8 * rows, dtype=bf16),
        in_specs=[SMEM] + [VMEM] * 6,
        out_specs=VMEM,
        scratch_shapes=[pltpu.VMEM((2, rows, features.shape[1] // 4), f32)],
        name="arrange",
        cost_estimate=pl.CostEstimate(flops=0, bytes_accessed=1 << 20, transcendentals=0),
    )(ids, features, fresh, *blocks, crossed)
    new_queue = pl.pallas_call(
        enqueue_body,
        out_shape=shape(slots, width, dtype=bf16),
        in_specs=[SMEM] + [VMEM] * 6,
        out_specs=VMEM,
        scratch_shapes=[pltpu.VMEM((slots, width), f32)],
        name="enqueue",
        cost_estimate=pl.CostEstimate(flops=4 * slots * rows * width * 2, bytes_accessed=2 << 20, transcendentals=0),
    )(ids, queue, fresh, *blocks, crossed)
    (grads,) = call(
        grad_body,
        [shape(rows + 16, width, dtype=bf16)],
        [ids, *queries, numer, denom, *received, positives_row, fresh, *blocks, crossed],
        "grad",
        flops=2 * 8 * rows * rows * width,
    )
    plane = {(dx, dy): grads if dx + dy == 0 else move(grads, dy * 2, dx) for dx in range(2) for dy in range(2)}
    pieces = []
    for dx in range(2):
        for dy in range(2):
            pieces += [plane[dx, dy], move(plane[dx, dy], 1, 0)]
    weight_grad, loss = call(
        final_body,
        [shape(features.shape[1] // 8, width), shape(1, rows)],
        [ids, turned, *pieces],
        "final",
        flops=2 * 8 * rows * width * features.shape[1] // 8,
    )
    return loss.reshape(rows), weight_grad, new_queue


def general(features, weight, queue, fresh_keys, positives, write_slot):
    projected = lax.psum(jnp.dot(features, weight, preferred_element_type=f32), "group")
    length = jnp.sqrt(jnp.sum(projected * projected, axis=1, keepdims=True) + epsilon)
    unit_rows = projected / length
    query_rows = unit_rows.astype(bf16)
    all_fresh = lax.all_gather(fresh_keys, "blk", axis=0, tiled=True)
    all_queries = lax.all_gather(query_rows, "blk", axis=0, tiled=True)
    query_total, key_width = all_queries.shape
    block_rows = 512
    query_blocks = all_queries.reshape(query_total // block_rows, block_rows, key_width)

    def score_block(carry, rows_now):
        similarity = jnp.einsum("qc,sc->qs", rows_now, queue, preferred_element_type=f32)
        e = jnp.exp(inverse_sharpness_factor * similarity)
        return carry, (jnp.dot(e.astype(bf16), queue, preferred_element_type=f32), jnp.sum(e, axis=1))

    _, (numer, denom) = lax.scan(score_block, jnp.float32(0.0), query_blocks)
    numer = lax.psum_scatter(numer.reshape(query_total, key_width), "blk", scatter_dimension=0, tiled=True)
    denom = lax.psum_scatter(denom.reshape(query_total), "blk", scatter_dimension=0, tiled=True)
    numerator, denominator = lax.psum((numer, denom), "group")
    paired = jnp.take(all_fresh, positives, axis=0).astype(f32)
    pair_score = inverse_sharpness_factor * jnp.sum(query_rows.astype(f32) * paired, axis=1)
    pair_weight = jnp.exp(pair_score)
    mass = pair_weight + denominator
    query_loss = jnp.log(mass) - pair_score
    slope = inverse_sharpness_factor * ((pair_weight[:, None] * paired + numerator) / mass[:, None] - paired)
    along = jnp.sum(slope * unit_rows, axis=1, keepdims=True)
    grad_projected = ((slope - along * unit_rows) / length).astype(bf16)
    weight_grad = lax.psum_scatter(
        lax.dot_general(features, grad_projected, (((0,), (0,)), ((), ())), preferred_element_type=f32),
        "blk",
        scatter_dimension=0,
        tiled=True,
    )
    slot_count = queue.shape[0]
    device = lax.axis_index("group") * lax.axis_size("blk") + lax.axis_index("blk")
    offset = device * slot_count + jnp.arange(slot_count, dtype=jnp.int32) - write_slot[0]
    inside = (offset >= 0) & (offset < query_total)
    picked = jnp.take(all_fresh, jnp.clip(offset, 0, query_total - 1), axis=0)
    return query_loss, weight_grad, jnp.where(inside[:, None], picked, queue)


def solution(mesh):
    in_specs = (
        P("blk", "group"),
        P("group", None),
        P(("group", "blk"), None),
        P("blk", None),
        P("blk"),
        P(),
    )
    out_specs = (P("blk"), P(("group", "blk"), None), P(("group", "blk"), None))

    def local(features, weight, queue, fresh_keys, positives, write_slot):
        fits = (
            mesh.shape["group"] == 4
            and mesh.shape["blk"] == 8
            and fresh_keys.shape[0] == 128
            and features.shape[1] == 512
            and queue.shape[1] == 256
        )
        body = fast if fits else general
        return body(features, weight, queue, fresh_keys, positives, write_slot)

    return jax.shard_map(local, mesh=mesh, in_specs=in_specs, out_specs=out_specs, check_vma=False)
```

```python
import functools
import jax
import jax.numpy as jnp
from jax import lax
from jax.experimental import pallas as pl
from jax.experimental.pallas import tpu as pltpu
from jax.sharding import PartitionSpec as P


epsilon = 1e-06
inverse_sharpness_factor = 8.0
f32, bf16 = jnp.float32, jnp.bfloat16
VMEM = pl.BlockSpec(memory_space=pltpu.VMEM)
LIMIT = 16 << 20
SMEM = pl.BlockSpec(memory_space=pltpu.SMEM)


def call(body, outs, ins, name, flops=0):
    nbytes = sum(a.size * a.dtype.itemsize for a in ins) + sum(o.size * o.dtype.itemsize for o in outs)
    return pl.pallas_call(
        body,
        out_shape=outs,
        in_specs=[SMEM] + [VMEM] * (len(ins) - 1),
        out_specs=[VMEM] * len(outs),
        name=name,
        compiler_params=pltpu.CompilerParams(vmem_limit_bytes=LIMIT),
        cost_estimate=pl.CostEstimate(flops=flops, bytes_accessed=nbytes, transcendentals=0),
    )(*ins)


def shape(*dims, dtype=f32):
    return jax.ShapeDtypeStruct(dims, dtype)


def dot(a, b):
    return jnp.dot(a, b, preferred_element_type=f32)


def row_block(lo_row, hi_row):
    n = lo_row.shape[1]
    first = lax.broadcasted_iota(jnp.int32, (16, n), 0) == 0
    parts = [jnp.where(first, jnp.broadcast_to(v, (16, n)), 0.0).astype(bf16) for v in (lo_row, hi_row)]
    return jnp.concatenate(parts, axis=1)


def split_row(row):
    high = row.astype(bf16).astype(f32)
    return high, row - high


def as_row(col):
    n = col.shape[0]
    return jnp.transpose(jnp.broadcast_to(col, (n, n)))[0:1, :]


def as_column(row):
    n = row.shape[1]
    return jnp.transpose(jnp.broadcast_to(row, (n, n)))[:, 0:1]


def prep_body(ids, features, weight, fresh, positives, keep, send, *rest):
    messages, scratch = rest[:-1], rest[-1]
    z, core = ids[0], ids[1]
    rows, width = fresh.shape
    half = rows // 2
    scratch[...] = dot(features[...], weight[...])
    keep[...] = scratch[pl.ds(pl.multiple_of(core * half, half), half), :]
    send[...] = scratch[pl.ds(pl.multiple_of((1 - core) * half, half), half), :]
    cols = features.shape[1] // (len(messages) + 1)
    index = positives[...]
    tail = row_block(
        lax.shift_right_logical(index, 7).astype(f32), lax.bitwise_and(index, 127).astype(f32)
    )
    for k, message in enumerate(messages, 1):
        peer = lax.bitwise_xor(z, k)
        message[0:rows, 0:width] = fresh[...]
        message[0:rows, width:] = features[:, pl.ds(pl.multiple_of(peer * cols, cols), cols)]
        message[rows:, 0:width] = tail
        message[rows:, width:] = jnp.zeros((16, cols), bf16)


def halve_body(ids, keep, got, own, send):
    quarter = own.shape[0]
    y = ids[0]
    for ref, at in ((own, y), (send, 1 - y)):
        rows = pl.ds(pl.multiple_of(at * quarter, quarter), quarter)
        ref[...] = keep[rows, :] + got[rows, :]


def pack_pair(first, second, x):
    half = first.shape[1] // 2
    low = jnp.concatenate([first[:, :half], second[:, :half]], axis=1)
    high = jnp.concatenate([first[:, half:], second[:, half:]], axis=1)
    return jnp.where(x == 0, low, high)


def feature_blocks(ids, features, messages, rows, width):
    z = ids[0]
    cols = features.shape[1] // (len(messages) + 1)
    own = features[:, pl.ds(pl.multiple_of(z * cols, cols), cols)]
    return [own.astype(f32)] + [m[0:rows, width:].astype(f32) for m in messages]


def cross_body(ids, features, fresh, *rest):
    messages, out = rest[:-1], rest[-1]
    rows, width = fresh.shape
    other = 1 - ids[1]
    blocks = feature_blocks(ids, features, messages, rows, width)
    for k, ref in enumerate((fresh, *messages)):
        out[:, k * width : (k + 1) * width] = ref[0:rows, 0:width]
    base = len(blocks) * width
    lanes = blocks[0].shape[1]
    for k in range(0, len(blocks), 2):
        pair = pack_pair(blocks[k], blocks[k + 1], other).astype(bf16)
        out[:, base + k // 2 * lanes : base + (k // 2 + 1) * lanes] = pair


def arrange_body(ids, features, fresh, *rest):
    messages, crossed, out, scratch = rest[:-3], rest[-3], rest[-2], rest[-1]
    rows, width = fresh.shape
    x, y, core = ids[1], ids[2], ids[3]
    quarter = rows // 4
    blocks = feature_blocks(ids, features, messages, rows, width)
    lanes = blocks[0].shape[1]
    base = len(blocks) * width
    per_z = 8 * quarter
    for k in range(0, len(blocks), 2):
        scratch[0] = pack_pair(blocks[k], blocks[k + 1], x)
        scratch[1] = crossed[:, base + k // 2 * lanes : base + (k // 2 + 1) * lanes].astype(f32)
        picked = []
        for dx in range(2):
            for dy in range(2):
                for dc in range(2):
                    at = lax.bitwise_xor(core, dc) * 2 + lax.bitwise_xor(y, dy)
                    picked.append(scratch[dx, pl.ds(pl.multiple_of(at * quarter, quarter), quarter), :])
        turned = jnp.transpose(jnp.concatenate(picked, axis=0)).astype(bf16)
        out[:, k * per_z : (k + 1) * per_z] = turned[0 : lanes // 2]
        out[:, (k + 1) * per_z : (k + 2) * per_z] = turned[lanes // 2 :]


def unit_of(projected):
    length = jnp.sqrt(jnp.sum(projected * projected, axis=1, keepdims=True) + epsilon)
    return projected / length, length


def score_body(ids, *refs):
    queries, keys, (message, numer_out, denom_out) = refs[:4], refs[4:-3], refs[-3:]
    projected = jnp.concatenate([q[...] for q in queries], axis=0)
    query = unit_of(projected)[0].astype(bf16)
    count, width = projected.shape
    numer = jnp.zeros((count, width), f32)
    denom = jnp.zeros((count, 1), f32)
    for block in keys:
        key = block[...]
        similarity = lax.dot_general(query, key, (((1,), (1,)), ((), ())), preferred_element_type=f32)
        e = jnp.exp(inverse_sharpness_factor * similarity)
        denom = denom + jnp.sum(e, axis=1, keepdims=True)
        numer = numer + dot(e.astype(bf16), key)
    numer_out[...] = numer
    denom_out[...] = jnp.broadcast_to(denom, denom_out.shape)
    message[0:count, :] = numer.astype(bf16)
    message[count:, :] = row_block(*split_row(as_row(denom)))


def grad_body(ids, *refs):
    queries, numer_ref, denom_ref = refs[:4], refs[4], refs[5]
    messages, (positives, fresh), blocks, crossed, out = refs[6:9], refs[9:11], refs[11:14], refs[14], refs[15]
    z, x, quarter_at = ids[0], ids[1], ids[4]
    projected = jnp.concatenate([q[...] for q in queries], axis=0)
    count, width = projected.shape
    quarter = count // 4
    unit, length = unit_of(projected)
    query = unit.astype(bf16).astype(f32)
    numer = numer_ref[...]
    denom = denom_ref[:, 0:1]
    for j, message in enumerate(messages, 1):
        part = message[0:count, :].astype(f32)
        row = message[count : count + 16, :].astype(f32)[0:1, :]
        column = as_column(row[:, :count] + row[:, count:])
        order = [j ^ k for k in range(4)]
        numer = numer + jnp.concatenate([part[k * quarter : (k + 1) * quarter] for k in order], axis=0)
        denom = denom + jnp.concatenate([column[k * quarter : (k + 1) * quarter] for k in order], axis=0)
    lanes = lax.broadcasted_iota(jnp.int32, (1, count), 1)
    tables = [positives[...].astype(f32)]
    for block in blocks:
        row = block[count : count + 16, 0:width].astype(f32)[0:1, :]
        tables.append(row[:, :count] * 128.0 + row[:, count:])
    columns = []
    for table in tables:
        column = jnp.transpose(jnp.broadcast_to(table, (count, count)))
        picked = jnp.zeros((quarter, 1), f32)
        for at in range(4):
            picked = jnp.where(quarter_at == at, column[at * quarter : (at + 1) * quarter, 0:1], picked)
        columns.append(picked)
    index = jnp.concatenate(columns, axis=0).astype(jnp.int32)
    slots = lax.broadcasted_iota(jnp.int32, (count, count), 1)
    positive = jnp.zeros((count, width), f32)
    for k in range(4):
        for dx in range(2):
            base = (lax.bitwise_xor(z, k) * 2 + lax.bitwise_xor(x, dx)) * count
            hot = (slots + base == index).astype(f32).astype(bf16)
            if dx == 1:
                rows = crossed[:, k * width : (k + 1) * width]
            else:
                rows = fresh[...] if k == 0 else blocks[k - 1][0:count, 0:width]
            positive = positive + dot(hot, rows)
    score = inverse_sharpness_factor * jnp.sum(query * positive, axis=1, keepdims=True)
    weight = jnp.exp(score)
    mass = weight + denom
    loss = jnp.log(mass) - score
    slope = inverse_sharpness_factor * ((weight * positive + numer) / mass - positive)
    along = jnp.sum(slope * unit, axis=1, keepdims=True)
    out[0:count, :] = ((slope - along * unit) / length).astype(bf16)
    out[count:, :] = row_block(*split_row(as_row(loss)))


def final_body(ids, *refs):
    turned, pieces, (grad, loss_out) = refs[0], refs[1:9], refs[9:]
    y, core = ids[2], ids[3]
    count = pieces[0].shape[0] - 16
    quarter = count // 4
    total = None
    for m in range(4):
        rows = jnp.concatenate([p[m * quarter : (m + 1) * quarter, :] for p in pieces], axis=0)
        term = dot(turned[:, m * 8 * quarter : (m + 1) * 8 * quarter], rows)
        total = term if total is None else total + term
    grad[...] = total
    place = lax.broadcasted_iota(jnp.int32, (1, count), 1) // quarter
    loss = jnp.zeros((1, count), f32)
    for dy in range(2):
        for dc in range(2):
            row = pieces[dy * 2 + dc][count : count + 16, :].astype(f32)[0:1, :]
            value = (row[:, :count] + row[:, count:])[:, :quarter]
            at = lax.bitwise_xor(core, dc) * 2 + lax.bitwise_xor(y, dy)
            loss = jnp.where(place == at, jnp.concatenate([value] * 4, axis=1), loss)
    loss_out[...] = loss


def enqueue_body(ids, queue, fresh, m1, m2, m3, crossed, out, scratch):
    z, x, start = ids[0], ids[1], ids[5]
    slots, width = queue.shape
    rows = fresh.shape[0]
    total = 8 * rows
    out[...] = queue[...]
    @pl.when((start < total) & (start + slots > 0))
    def _():
        scratch[...] = jnp.zeros((slots, width), f32)
        offset = lax.broadcasted_iota(jnp.int32, (slots, rows), 0) + start
        place = lax.broadcasted_iota(jnp.int32, (slots, rows), 1)
        for k in range(4):
            for dx in range(2):
                base = (lax.bitwise_xor(z, k) * 2 + lax.bitwise_xor(x, dx)) * rows

                @pl.when((start < base + rows) & (start + slots > base))
                def _():
                    hot = (place + base == offset).astype(f32).astype(bf16)
                    if dx == 1:
                        values = crossed[:, k * width : (k + 1) * width]
                    else:
                        values = fresh[...] if k == 0 else (m1, m2, m3)[k - 1][0:rows, 0:width]
                    scratch[...] += dot(hot, values)

        at = lax.broadcasted_iota(jnp.int32, (slots, width), 0) + start
        inside = (at >= 0) & (at < total)
        out[...] = jnp.where(inside, scratch[...], queue[...].astype(f32)).astype(bf16)


def fast(features, weight, queue, fresh, positives, write_slot):
    group, blk = lax.axis_index("group"), lax.axis_index("blk")
    groups, blks = lax.axis_size("group"), lax.axis_size("blk")
    y, core, z, x = group // 2, group % 2, blk // 2, blk % 2
    rows, width = fresh.shape
    slots = queue.shape[0]
    device = group * blks + blk
    start = device * slots - write_slot[0]
    ids = jnp.stack([z, x, y, core, core * 2 + y, start]).astype(jnp.int32)

    def move(value, dg, db):
        pairs = [
            (g * blks + b, (g ^ dg) * blks + (b ^ db)) for g in range(groups) for b in range(blks)
        ]
        return lax.ppermute(value, ("group", "blk"), pairs)

    keys = [queue] + [move(queue, dy * 2, dx) for dy, dx in ((0, 1), (1, 0), (1, 1))]
    keys += [move(k, 1, 0) for k in keys]

    positives_row = positives.reshape(1, rows)
    prep = pl.pallas_call(
        prep_body,
        out_shape=[shape(rows // 2, width)] * 2 + [shape(rows + 16, width + features.shape[1] // 4, dtype=bf16)] * 3,
        in_specs=[SMEM] + [VMEM] * 4,
        out_specs=[VMEM] * 5,
        scratch_shapes=[pltpu.VMEM((rows, width), f32)],
        name="prep",
        compiler_params=pltpu.CompilerParams(vmem_limit_bytes=LIMIT),
        cost_estimate=pl.CostEstimate(flops=2 * rows * width * features.shape[1], bytes_accessed=1 << 20, transcendentals=0),
    )
    keep, send, *outgoing = prep(jnp.stack([z, core]).astype(jnp.int32), features, weight, fresh, positives_row)
    blocks = [move(m, 0, 2 * k) for k, m in enumerate(outgoing, 1)]
    got = move(send, 1, 0)
    own, send = call(halve_body, [shape(rows // 4, width)] * 2, [ids[2:3], keep, got], "halve")
    own = own + move(send, 2, 0)
    queries = [own] + [move(own, 0, 2 * k) for k in (1, 2, 3)]

    crossed = move(
        call(cross_body, [shape(rows, 4 * width + features.shape[1] // 2, dtype=bf16)], [ids, features, fresh, *blocks], "cross")[0],
        0,
        1,
    )
    message, numer, denom = call(
        score_body,
        [shape(rows + 16, width, dtype=bf16), shape(rows, width), shape(rows, rows)],
        [ids, *queries, *keys],
        "score",
        flops=4 * rows * width * 8 * slots,
    )
    received = [move(message, 0, 2 * k) for k in (1, 2, 3)]
    turned = pl.pallas_call(
        arrange_body,
        out_shape=shape(features.shape[1] // 8, 8 * rows, dtype=bf16),
        in_specs=[SMEM] + [VMEM] * 6,
        out_specs=VMEM,
        scratch_shapes=[pltpu.VMEM((2, rows, features.shape[1] // 4), f32)],
        name="arrange",
        compiler_params=pltpu.CompilerParams(vmem_limit_bytes=LIMIT),
        cost_estimate=pl.CostEstimate(flops=0, bytes_accessed=1 << 20, transcendentals=0),
    )(ids, features, fresh, *blocks, crossed)
    new_queue = pl.pallas_call(
        enqueue_body,
        out_shape=shape(slots, width, dtype=bf16),
        in_specs=[SMEM] + [VMEM] * 6,
        out_specs=VMEM,
        scratch_shapes=[pltpu.VMEM((slots, width), f32)],
        name="enqueue",
        compiler_params=pltpu.CompilerParams(vmem_limit_bytes=LIMIT),
        cost_estimate=pl.CostEstimate(flops=4 * slots * rows * width * 2, bytes_accessed=2 << 20, transcendentals=0),
    )(ids, queue, fresh, *blocks, crossed)
    (grads,) = call(
        grad_body,
        [shape(rows + 16, width, dtype=bf16)],
        [ids, *queries, numer, denom, *received, positives_row, fresh, *blocks, crossed],
        "grad",
        flops=2 * 8 * rows * rows * width,
    )
    plane = {(dx, dy): grads if dx + dy == 0 else move(grads, dy * 2, dx) for dx in range(2) for dy in range(2)}
    pieces = []
    for dx in range(2):
        for dy in range(2):
            pieces += [plane[dx, dy], move(plane[dx, dy], 1, 0)]
    weight_grad, loss = call(
        final_body,
        [shape(features.shape[1] // 8, width), shape(1, rows)],
        [ids, turned, *pieces],
        "final",
        flops=2 * 8 * rows * width * features.shape[1] // 8,
    )
    return loss.reshape(rows), weight_grad, new_queue


def general(features, weight, queue, fresh_keys, positives, write_slot):
    projected = lax.psum(jnp.dot(features, weight, preferred_element_type=f32), "group")
    length = jnp.sqrt(jnp.sum(projected * projected, axis=1, keepdims=True) + epsilon)
    unit_rows = projected / length
    query_rows = unit_rows.astype(bf16)
    all_fresh = lax.all_gather(fresh_keys, "blk", axis=0, tiled=True)
    all_queries = lax.all_gather(query_rows, "blk", axis=0, tiled=True)
    query_total, key_width = all_queries.shape
    block_rows = 512
    query_blocks = all_queries.reshape(query_total // block_rows, block_rows, key_width)

    def score_block(carry, rows_now):
        similarity = jnp.einsum("qc,sc->qs", rows_now, queue, preferred_element_type=f32)
        e = jnp.exp(inverse_sharpness_factor * similarity)
        return carry, (jnp.dot(e.astype(bf16), queue, preferred_element_type=f32), jnp.sum(e, axis=1))

    _, (numer, denom) = lax.scan(score_block, jnp.float32(0.0), query_blocks)
    numer = lax.psum_scatter(numer.reshape(query_total, key_width), "blk", scatter_dimension=0, tiled=True)
    denom = lax.psum_scatter(denom.reshape(query_total), "blk", scatter_dimension=0, tiled=True)
    numerator, denominator = lax.psum((numer, denom), "group")
    paired = jnp.take(all_fresh, positives, axis=0).astype(f32)
    pair_score = inverse_sharpness_factor * jnp.sum(query_rows.astype(f32) * paired, axis=1)
    pair_weight = jnp.exp(pair_score)
    mass = pair_weight + denominator
    query_loss = jnp.log(mass) - pair_score
    slope = inverse_sharpness_factor * ((pair_weight[:, None] * paired + numerator) / mass[:, None] - paired)
    along = jnp.sum(slope * unit_rows, axis=1, keepdims=True)
    grad_projected = ((slope - along * unit_rows) / length).astype(bf16)
    weight_grad = lax.psum_scatter(
        lax.dot_general(features, grad_projected, (((0,), (0,)), ((), ())), preferred_element_type=f32),
        "blk",
        scatter_dimension=0,
        tiled=True,
    )
    slot_count = queue.shape[0]
    device = lax.axis_index("group") * lax.axis_size("blk") + lax.axis_index("blk")
    offset = device * slot_count + jnp.arange(slot_count, dtype=jnp.int32) - write_slot[0]
    inside = (offset >= 0) & (offset < query_total)
    picked = jnp.take(all_fresh, jnp.clip(offset, 0, query_total - 1), axis=0)
    return query_loss, weight_grad, jnp.where(inside[:, None], picked, queue)


def solution(mesh):
    in_specs = (
        P("blk", "group"),
        P("group", None),
        P(("group", "blk"), None),
        P("blk", None),
        P("blk"),
        P(),
    )
    out_specs = (P("blk"), P(("group", "blk"), None), P(("group", "blk"), None))

    def local(features, weight, queue, fresh_keys, positives, write_slot):
        fits = (
            mesh.shape["group"] == 4
            and mesh.shape["blk"] == 8
            and fresh_keys.shape[0] == 128
            and features.shape[1] == 512
            and queue.shape[1] == 256
        )
        body = fast if fits else general
        return body(features, weight, queue, fresh_keys, positives, write_slot)

    return jax.shard_map(local, mesh=mesh, in_specs=in_specs, out_specs=out_specs, check_vma=False)
```
